128 devices in a mesh: tok: 32 (over z, x, y_hi), ch: 4 (over y_lo, core).
Axes of the slice: x: 4, y: 4 (y_hi: 2, y_lo: 2; y = y_hi * 2 + y_lo), z: 4, core: 2. Of those that a mesh axis runs over, the one named last changes fastest.
Arguments:
- tokens: bfloat16 [262144, 1024], P('tok', 'ch'), may hold values from -6 to 6
- w_value: bfloat16 [1024, 1024], P(None, 'ch'), may hold values from -0.1875 to 0.1875
- w_gate: bfloat16 [1024, 1024], P(None, 'ch'), may hold values from -0.1875 to 0.1875
- first_factor: bfloat16 [512, 512], replicated, may hold values from -0.25 to 0.25
- twiddle: float32 [512, 512], P('tok'), may hold values from 0.5 to 1.5
- second_factor: float32 [512, 512], replicated, may hold values from -0.25 to 0.25
- freq_kernel: float32 [512, 1024], P('tok', 'ch'), may hold values from -5 to 5
- row_kernel: float32 [512, 1024], P(None, 'ch'), may hold values from -5 to 5
- inverse_first: float32 [512, 512], replicated, may hold values from -0.25 to 0.25
- inverse_second: float32 [512, 512], replicated, may hold values from -0.25 to 0.25
Outputs:
- mixed: bfloat16 [262144, 1024], P('tok', 'ch')
The draws below stay inside these ranges and needn't reach their ends.
All inputs are finite; a program needn't handle non-finite values.
Results may differ from the reference program's by a relative error of at most 0.0049.
Values may be sent and summed in bfloat16 or wider, within the bound.
A program may use at most 128 MiB of HBM per device.

```python
import math
import jax
import jax.numpy as jnp
from jax import lax

D = 1024
BLOCK_A = 512
BLOCK_B = 512
SEQ = 262144


def block_scale(rng, shape, cuts, low, top_value):
    def one(axis_at, shards_of):
        draws = jax.random.uniform(jax.random.fold_in(jax.random.fold_in(rng, 6), axis_at), (shards_of,), jnp.float32, low / len(cuts), top_value / len(cuts))
        return jnp.repeat(jnp.exp(draws), shape[axis_at] // shards_of).reshape((-1,) + (1,) * (len(shape) - axis_at - 1))

    level = one(*cuts[0])
    for cut in cuts[1:]:
        level = level * one(*cut)
    return level


def centred(own_key, dims, deviation, most, split=(), kind=jnp.bfloat16):
    values = deviation * jax.random.normal(own_key, dims, jnp.float32)
    if split:
        values = values * block_scale(own_key, dims, split, -0.22, 0.18)
    return jnp.clip(values, -most, most).astype(kind)


def setup_inputs(seed: int = 0) -> dict:
    key_list = jax.random.split(jax.random.key(seed), 11)
    return {
        "tokens": centred(key_list[0], (SEQ, D), 1.0, 6.0, ((0, 32), (1, 4))),
        "w_value": centred(key_list[1], (D, D), D ** -0.5, 0.1875, ((1, 4),)),
        "w_gate": centred(key_list[2], (D, D), D ** -0.5, 0.1875, ((1, 4),)),
        "first_factor": centred(key_list[3], (BLOCK_B, BLOCK_B), BLOCK_B ** -0.5, 0.25),
        "twiddle": jnp.clip(0.5 + 1.0 * jax.random.uniform(key_list[4], (BLOCK_A, BLOCK_B), jnp.float32) ** block_scale(key_list[4], (BLOCK_A, BLOCK_B), ((0, 32),), -0.2, 0.2), 0.5, 1.5),
        "second_factor": centred(key_list[5], (BLOCK_A, BLOCK_A), BLOCK_A ** -0.5, 0.25, (), jnp.float32),
        "freq_kernel": centred(key_list[6], (BLOCK_B, D), 1.0, 5.0, ((0, 32), (1, 4)), jnp.float32),
        "row_kernel": centred(key_list[7], (BLOCK_A, D), 1.0, 5.0, ((1, 4),), jnp.float32),
        "inverse_first": centred(key_list[8], (BLOCK_A, BLOCK_A), BLOCK_A ** -0.5, 0.25, (), jnp.float32),
        "inverse_second": centred(key_list[9], (BLOCK_B, BLOCK_B), BLOCK_B ** -0.5, 0.25, (), jnp.float32),
    }


def reference(tokens, w_value, w_gate, first_factor, twiddle, second_factor, freq_kernel, row_kernel, inverse_first, inverse_second):
    width = math.gcd(D, 128)
    count = D // width
    highest = lax.Precision.HIGHEST
    first_wide = first_factor.astype(jnp.float32)

    def split_cols(matrix):
        return matrix.reshape(matrix.shape[0], count, width).transpose(1, 0, 2)

    def one_block(pieces):
        value_cols, gate_cols, freq_cols, row_cols = pieces
        value = jnp.dot(tokens, value_cols, preferred_element_type=jnp.float32)
        gate = jnp.dot(tokens, gate_cols, preferred_element_type=jnp.float32)
        gated = (value * jax.nn.silu(gate)).astype(jnp.bfloat16).reshape(BLOCK_A, BLOCK_B, width)
        section = jnp.einsum('kb,abc->akc', first_wide, gated.astype(jnp.float32), precision=highest)
        section = section * twiddle[:, :, None]
        section = jnp.einsum('ja,akc->jkc', second_factor, section, precision=highest)
        section = section * freq_cols[None, :, :] * row_cols[:, None, :]
        section = jnp.einsum('ij,jkc->ikc', inverse_first, section, precision=highest)
        result = jnp.einsum('bk,akc->abc', inverse_second, section, precision=highest)
        return result.reshape(SEQ, width).astype(jnp.bfloat16)

    blocks = lax.map(one_block, (split_cols(w_value), split_cols(w_gate), split_cols(freq_kernel), split_cols(row_kernel)))
    return blocks.transpose(1, 0, 2).reshape(SEQ, D)
```

```python
import jax
import jax.numpy as jnp
from jax import lax
from jax.sharding import PartitionSpec as P

BLOCK_B = 512


def shards(
    tokens,
    w_value,
    w_gate,
    first_factor,
    twiddle,
    second_factor,
    freq_kernel,
    row_kernel,
    inverse_first,
    inverse_second,
):
    tok_rows, channels = tokens.shape
    n_tok, n_ch = lax.axis_size("tok"), lax.axis_size("ch")
    f32, bf16 = jnp.float32, jnp.bfloat16
    wide = channels * n_ch
    my_ch = lax.axis_index("ch")
    piece = lax.all_to_all(tokens, "ch", split_axis=0, concat_axis=1, tiled=True)
    weights = lax.all_gather(jnp.concatenate([w_value, w_gate], axis=1), "ch", axis=0)
    both = jnp.einsum("nd,hdc->nhc", piece, weights, preferred_element_type=f32)
    value, gate = both[:, :, :channels], both[:, :, channels:]
    rows = tok_rows // BLOCK_B // n_ch
    gated = (value * jax.nn.silu(gate)).astype(bf16).reshape(rows, BLOCK_B, wide)
    my_twiddle = lax.dynamic_slice_in_dim(twiddle, my_ch * rows, rows, 0)
    section = jnp.einsum("kb,abc->akc", first_factor, gated, preferred_element_type=f32)
    section = (section * my_twiddle[:, :, None]).astype(bf16)
    k_rows = BLOCK_B // n_tok
    section = section.reshape(rows, n_tok, k_rows, n_ch, channels).transpose(1, 3, 0, 2, 4)
    section = section.reshape(n_tok * n_ch, rows, k_rows, channels)
    section = lax.all_to_all(section, ("tok", "ch"), split_axis=0, concat_axis=0, tiled=True)
    section = section.reshape(n_tok * n_ch * rows, k_rows, channels)
    spectrum = jnp.einsum("ja,akc->jkc", second_factor.astype(bf16), section, preferred_element_type=f32)
    spectrum = (spectrum * freq_kernel[None, :, :] * row_kernel[:, None, :]).astype(bf16)
    spectrum = jnp.einsum("ij,jkc->ikc", inverse_first.astype(bf16), spectrum, preferred_element_type=f32)
    spectrum = lax.all_to_all(spectrum.astype(bf16), "tok", split_axis=0, concat_axis=1, tiled=True)
    result = jnp.einsum("bk,akc->abc", inverse_second.astype(bf16), spectrum, preferred_element_type=f32)
    return result.reshape(tok_rows, channels).astype(bf16)


def solution(mesh):
    return jax.shard_map(
        shards,
        mesh=mesh,
        in_specs=(
            P("tok", "ch"),
            P(None, "ch"),
            P(None, "ch"),
            P(),
            P("tok", None),
            P(),
            P("tok", "ch"),
            P(None, "ch"),
            P(),
            P(),
        ),
        out_specs=P("tok", "ch"),
        check_vma=False,
    )
```

```python
import functools

import jax
import jax.numpy as jnp
from jax import lax
from jax.experimental import pallas as pl
from jax.experimental.pallas import tpu as pltpu
from jax.sharding import PartitionSpec as P

MESH = pl.DeviceIdType.MESH
LANES = 128
F32, BF16 = jnp.float32, jnp.bfloat16


def dot(a, b):
    return jnp.dot(a, b, preferred_element_type=F32)


def mixer(
    n_tok,
    tokens, w_value, w_gate, first, twiddle, second, inv_one, inv_two, freq, row_kernel,
    out,
    x, w, sec_out, sec_in, wide_in, wide_out, spec_out, spec_in, result,
    wide_mats, mats,
    cross_s, cross_r, core_s, core_r, fwd_s, fwd_r, own_sem, w_sem, ws_sem, wr_sem, mat_sem,
    a_send, a_recv, a_own, b_send, b_recv, b_own, out_sem,
):
    t, h = lax.axis_index("tok"), lax.axis_index("ch")
    lo, core = h // 2, h % 2
    half, pieces, block, width = x.shape
    n_k = sec_in.shape[1]
    n_a = sec_in.shape[0]
    local = 2 * half
    y_dev = (t, (1 - lo) * 2 + core)
    core_dev = (t, lo * 2 + 1 - core)
    w_dev = (t + 1 - 2 * (t % 2), (1 - lo) * 2 + core)
    far, far_core, near = (1 - lo) * 2 + core, (1 - lo) * 2 + 1 - core, lo * 2 + 1 - core

    barrier = pltpu.get_barrier_semaphore()
    me = t * 2 + lo

    @pl.loop(1, 2 * n_tok)
    def _(j):
        p = (me + j) % (2 * n_tok)
        pl.semaphore_signal(barrier, inc=1, device_id=(p // 2, (p % 2) * 2 + core), device_id_type=MESH)

    pl.semaphore_signal(barrier, inc=1, device_id=core_dev, device_id_type=MESH)
    pl.semaphore_wait(barrier, 2 * n_tok)

    def remote(src, dst, s, r, dev):
        return pltpu.make_async_remote_copy(
            src_ref=src, dst_ref=dst, send_sem=s, recv_sem=r, device_id=dev, device_id_type=MESH
        )

    def rows(at, r):
        return tokens.at[pl.ds(pl.multiple_of((at * half + r) * block, block), block), :]

    def cross(r):
        return remote(rows(1 - lo, r), x.at[r, h], cross_s.at[r], cross_r.at[r], y_dev)

    def partner(r):
        return remote(rows(lo, r), x.at[r, h], core_s.at[r], core_r.at[r], core_dev)

    def own(r):
        return pltpu.make_async_copy(rows(lo, r), x.at[r, h], own_sem.at[r])

    def forward(r):
        return remote(x.at[r, far], x.at[r, far], fwd_s.at[r], fwd_r.at[r], core_dev)

    def w_own(i):
        return pltpu.make_async_copy((w_value, w_gate)[i], w.at[lo, i], w_sem.at[i])

    def w_far(i):
        return remote((w_value, w_gate)[i], w.at[lo, i], ws_sem.at[i], wr_sem.at[i], w_dev)

    def arrived(r, piece, sem):
        pltpu.make_async_copy(x.at[r, piece], x.at[r, piece], sem.at[r]).wait()

    for i in range(2):
        w_own(i).start()
        w_far(i).start()

    @pl.loop(0, half)
    def _(r):
        cross(r).start()
        own(r).start()
        partner(r).start()

    square = (second, inv_one, inv_two)
    for i in range(3):
        pltpu.make_async_copy(square[i], wide_mats.at[i], mat_sem.at[i]).start()
    for i in range(3):
        pltpu.make_async_copy(square[i], wide_mats.at[i], mat_sem.at[i]).wait()
        mats[i] = wide_mats[i].astype(BF16)
    for i in range(2):
        w_own(i).wait()

    tw_lane = lax.broadcasted_iota(jnp.int32, twiddle.shape, 1)

    def project(step):
        q = half // 2
        early = step < q
        middle = (step >= q) & (step < 2 * q)
        late = step - 2 * q
        r = jnp.where(early, step, jnp.where(middle, step - q, q + late // 2))
        other = jnp.where(early, 0, jnp.where(middle, 1, late % 2))
        l = lo + other - 2 * lo * other

        @pl.when(step == q)
        def _():
            for i in range(2):
                pltpu.make_async_copy(w.at[1 - lo, i], w.at[1 - lo, i], wr_sem.at[i]).wait()

        @pl.when(other == 0)
        def _():
            arrived(r, far, cross_r)
            forward(r).start()
            own(r).wait()
            arrived(r, near, core_r)
            arrived(r, far_core, fwd_r)

        row = jnp.concatenate([x[r, p] for p in range(pieces)], axis=1)
        value = dot(row, w[l, 0])
        gate = dot(row, w[l, 1])
        gated = (value * (gate / (1.0 + jnp.exp(-gate)))).astype(BF16)
        scale = jnp.sum(jnp.where(tw_lane == lo * half + r, twiddle[...], 0.0), axis=1, keepdims=True)
        sec_out[r, l] = (dot(first[...], gated) * scale).astype(BF16)

        @pl.when(other == 1)
        def _():
            to = t * local + lo * half + r

            @pl.loop(1, 2 * n_tok)
            def _(j):
                p = (me + j * 27) % (2 * n_tok)
                pt, pl_ = p // 2, p % 2
                remote(
                    sec_out.at[r, pl_, pl.ds(pl.multiple_of(pt * n_k, n_k), n_k), :],
                    sec_in.at[to], a_send, a_recv, (pt, pl_ * 2 + core),
                ).start()

            pltpu.make_async_copy(
                sec_out.at[r, lo, pl.ds(pl.multiple_of(t * n_k, n_k), n_k), :], sec_in.at[to], a_own
            ).start()

    pl.loop(0, 2 * half)(project)

    pltpu.make_async_copy(sec_in.at[pl.ds(0, half)], sec_in.at[pl.ds(0, half)], a_own).wait()
    most = n_a - half
    pltpu.make_async_copy(sec_in.at[pl.ds(0, most)], sec_in.at[pl.ds(0, most)], a_recv).wait()

    step_a = 32
    n_half = width // LANES

    def spread(q):
        lanes = pl.ds(pl.multiple_of(q * LANES, LANES), LANES)

        @pl.loop(0, n_a // step_a)
        def _(i):
            part = sec_in[pl.ds(i * step_a, step_a), :, lanes].astype(F32)
            wide_in[pl.ds(pl.multiple_of(i * step_a * n_k, step_a * n_k), step_a * n_k), :] = part.reshape(
                step_a * n_k, LANES
            )

        @pl.loop(0, n_k // 2)
        def _(kp):
            two = [wide_in[pl.ds(2 * kp + i, n_a, stride=n_k), :].astype(BF16) for i in range(2)]
            mid = dot(mats[0], jnp.concatenate(two, axis=1))
            scale = [freq[2 * kp + i, q] * row_kernel[:, lanes] for i in range(2)]
            mid = (mid * jnp.concatenate(scale, axis=1)).astype(BF16)
            end = dot(mats[1], mid)
            for i in range(2):
                wide_out[pl.ds(2 * kp + i, n_a, stride=n_k), :] = end[:, i * LANES : (i + 1) * LANES]

        @pl.loop(0, n_tok)
        def _(j):
            pt = (t + j * 13) % n_tok
            rows_out = pl.ds(pl.multiple_of(pt * local, local), local)
            flat = pl.ds(pl.multiple_of(pt * local * n_k, local * n_k), local * n_k)
            spec_out[q, rows_out] = wide_out[flat, :].astype(BF16).reshape(local, n_k, LANES)
            at = pl.ds(pl.multiple_of(t * n_k, n_k), n_k)

            @pl.when(j > 0)
            def _():
                remote(
                    spec_out.at[q, rows_out], spec_in.at[q, :, at, :], b_send.at[q], b_recv.at[q], (pt, h)
                ).start()

            @pl.when(j == 0)
            def _():
                pltpu.make_async_copy(spec_out.at[q, rows_out], spec_in.at[q, :, at, :], b_own.at[q]).start()

    pl.loop(0, n_half)(spread)

    def finish(q):
        lanes = pl.ds(pl.multiple_of(q * LANES, LANES), LANES)
        mine = pl.ds(0, n_k)
        rest = pl.ds(0, (n_tok - 1) * n_k)
        pltpu.make_async_copy(spec_in.at[q, :, mine, :], spec_in.at[q, :, mine, :], b_own.at[q]).wait()
        pltpu.make_async_copy(spec_in.at[q, :, rest, :], spec_in.at[q, :, rest, :], b_recv.at[q]).wait()

        @pl.loop(0, local // 2)
        def _(ip):
            two = jnp.concatenate([spec_in[q, 2 * ip + i] for i in range(2)], axis=1)
            got = dot(mats[2], two).astype(BF16)
            for i in range(2):
                at = pl.ds(pl.multiple_of((2 * ip + i) * block, block), block)
                result[at, lanes] = got[:, i * LANES : (i + 1) * LANES]

            @pl.when(q == n_half - 1)
            def _():
                both = pl.ds(pl.multiple_of(2 * ip * block, 2 * block), 2 * block)
                pltpu.make_async_copy(result.at[both], out.at[both], out_sem.at[ip]).start()

    pl.loop(0, n_half)(finish)

    @pl.loop(0, half)
    def _(r):
        cross(r).wait_send()
        partner(r).wait_send()
        forward(r).wait_send()

    for i in range(2):
        w_far(i).wait_send()
    sent = pl.ds(0, most)
    pltpu.make_async_copy(sec_in.at[sent], sec_in.at[sent], a_send).wait()
    for q in range(n_half):
        gone = pl.ds(0, (n_tok - 1) * local)
        pltpu.make_async_copy(spec_out.at[q, gone], spec_out.at[q, gone], b_send.at[q]).wait()

    @pl.loop(0, local // 2)
    def _(ip):
        both = pl.ds(pl.multiple_of(2 * ip * block, 2 * block), 2 * block)
        pltpu.make_async_copy(result.at[both], out.at[both], out_sem.at[ip]).wait()


def shards(
    tokens,
    w_value,
    w_gate,
    first_factor,
    twiddle,
    second_factor,
    freq_kernel,
    row_kernel,
    inverse_first,
    inverse_second,
):
    n_tok = lax.axis_size("tok")
    tok_rows, width = tokens.shape
    block = first_factor.shape[0]
    depth = w_value.shape[0]
    n_a = second_factor.shape[0]
    local = tok_rows // block
    half = local // 2
    n_k = block // n_tok
    n_half = width // LANES
    hbm, vmem = pl.BlockSpec(memory_space=pl.ANY), pl.BlockSpec(memory_space=pltpu.VMEM)
    dma = pltpu.SemaphoreType.DMA
    return pl.pallas_call(
        functools.partial(mixer, n_tok),
        out_shape=jax.ShapeDtypeStruct((tok_rows, width), BF16),
        in_specs=[hbm, hbm, hbm, vmem, vmem, hbm, hbm, hbm, vmem, vmem],
        out_specs=hbm,
        scratch_shapes=[
            pltpu.VMEM((half, depth // width, block, width), BF16),
            pltpu.VMEM((2, 2, depth, width), BF16),
            pltpu.VMEM((half, 2, block, width), BF16),
            pltpu.VMEM((n_a, n_k, width), BF16),
            pltpu.VMEM((n_a * n_k, LANES), F32),
            pltpu.VMEM((n_a * n_k, LANES), F32),
            pltpu.VMEM((n_half, n_a, n_k, LANES), BF16),
            pltpu.VMEM((n_half, local, block, LANES), BF16),
            pltpu.VMEM((tok_rows, width), BF16),
            pltpu.VMEM((3, n_a, n_a), F32),
            pltpu.VMEM((3, n_a, n_a), BF16),
            dma((half,)), dma((half,)), dma((half,)), dma((half,)), dma((half,)), dma((half,)), dma((half,)),
            dma((2,)), dma((2,)), dma((2,)), dma((3,)),
            dma, dma, dma, dma((n_half,)), dma((n_half,)), dma((n_half,)), dma((local // 2,)),
        ],
        compiler_params=pltpu.CompilerParams(
            collective_id=0, has_side_effects=True, vmem_limit_bytes=62 * 2**20
        ),
    )(
        tokens, w_value, w_gate, first_factor, twiddle.T, second_factor, inverse_first, inverse_second,
        freq_kernel.reshape(n_k, n_half, 1, LANES), row_kernel,
    )


def solution(mesh):
    return jax.shard_map(
        shards,
        mesh=mesh,
        in_specs=(
            P("tok", "ch"),
            P(None, "ch"),
            P(None, "ch"),
            P(),
            P("tok", None),
            P(),
            P("tok", "ch"),
            P(None, "ch"),
            P(),
            P(),
        ),
        out_specs=P("tok", "ch"),
        check_vma=False,
    )
```

```python
import functools

import jax
import jax.numpy as jnp
from jax import lax
from jax.experimental import pallas as pl
from jax.experimental.pallas import tpu as pltpu
from jax.sharding import PartitionSpec as P

MESH = pl.DeviceIdType.MESH
LANES = 128
F32, BF16 = jnp.float32, jnp.bfloat16


def dot(a, b):
    return jnp.dot(a, b, preferred_element_type=F32)


def flip(index, bit):
    return index + bit - 2 * bit * ((index // bit) % 2)


def mixer(
    n_tok,
    tokens, w_value, w_gate, first, twiddle, second, inv_one, inv_two, freq, row_kernel,
    out,
    x, w, sec_out, sec_in, wide_in, wide_out, spec_out, spec_in, result,
    wide_mats, mats, first_mat, twiddle_raw, twiddle_cols, freq_raw, freq_rows, row_mat,
    cross_s, cross_r, core_s, core_r, fwd_s, fwd_r, own_sem, w_sem, ws_sem, wr_sem, small_sem,
    known, a_send, a_recv, a_own, b_send, b_recv, b_own, out_sem,
):
    t, h = lax.axis_index("tok"), lax.axis_index("ch")
    lo, core = h // 2, h % 2
    half, pieces, block, width = x.shape
    n_half, n_a, n_k, _ = sec_in.shape
    local = 2 * half
    me = t * 2 + lo
    y_dev = (t, flip(h, 2))
    core_dev = (t, flip(h, 1))
    w_dev = (flip(t, 1), flip(h, 2))
    far, far_core, near = flip(h, 2), flip(flip(h, 2), 1), flip(h, 1)
    bits = [2**i for i in range(n_tok.bit_length() - 1)]
    links = [y_dev] + [(flip(t, b), h) for b in bits]

    barrier = pltpu.get_barrier_semaphore()
    close = links + [core_dev, w_dev]
    for d in close:
        pl.semaphore_signal(barrier, inc=1, device_id=d, device_id_type=MESH)

    def remote(src, dst, s, r, dev):
        return pltpu.make_async_remote_copy(
            src_ref=src, dst_ref=dst, send_sem=s, recv_sem=r, device_id=dev, device_id_type=MESH
        )

    def rows(at, r):
        return tokens.at[pl.ds(pl.multiple_of((at * half + r) * block, block), block), :]

    def cross(r):
        return remote(rows(1 - lo, r), x.at[r, h], cross_s.at[r], cross_r.at[r], y_dev)

    def partner(r):
        return remote(rows(lo, r), x.at[r, h], core_s.at[r], core_r.at[r], core_dev)

    def own(r):
        return pltpu.make_async_copy(rows(lo, r), x.at[r, h], own_sem.at[r])

    def forward(r):
        return remote(x.at[r, far], x.at[r, far], fwd_s.at[r], fwd_r.at[r], core_dev)

    def w_own(i):
        return pltpu.make_async_copy((w_value, w_gate)[i], w.at[lo, i], w_sem.at[i])

    def w_far(i):
        return remote((w_value, w_gate)[i], w.at[lo, i], ws_sem.at[i], wr_sem.at[i], w_dev)

    def arrived(r, piece, sem):
        pltpu.make_async_copy(x.at[r, piece], x.at[r, piece], sem.at[r]).wait()

    small = [
        (twiddle, twiddle_raw), (first, first_mat), (freq, freq_raw), (second, wide_mats.at[0]),
        (inv_one, wide_mats.at[1]), (inv_two, wide_mats.at[2]), (row_kernel, row_mat),
    ]
    loads = [pltpu.make_async_copy(a, b, small_sem.at[i]) for i, (a, b) in enumerate(small)]
    for i in range(2):
        w_own(i).start()
    for load in loads:
        load.start()

    pl.semaphore_wait(barrier, len(close))

    @pl.loop(0, half)
    def _(r):
        cross(r).start()

    for i in range(2):
        w_far(i).start()

    @pl.loop(0, half)
    def _(r):
        own(r).start()
        partner(r).start()

    for i, d in enumerate(links):
        pl.semaphore_signal(known.at[i], inc=1, device_id=d, device_id_type=MESH)
        pl.semaphore_wait(known.at[i], 1)

    for load in loads:
        load.wait()
    same = lax.broadcasted_iota(jnp.int32, (block, block), 0) == lax.broadcasted_iota(
        jnp.int32, (block, block), 1
    )

    @pl.loop(0, half)
    def _(r):
        row = twiddle_raw[pl.ds(pl.multiple_of(lo * half, half), half), :]
        pick = lax.broadcasted_iota(jnp.int32, row.shape, 0) == r
        row = jnp.sum(jnp.where(pick, row, 0.0), axis=0, keepdims=True)
        column = jnp.sum(jnp.where(same, row, 0.0), axis=1, keepdims=True)
        twiddle_cols[r] = jnp.broadcast_to(column, (block, LANES))

    for k in range(n_k):
        for q in range(n_half):
            freq_rows[k, q] = freq_raw[k : k + 1, q * LANES : (q + 1) * LANES]
    for i in range(3):
        high = wide_mats[i].astype(BF16)
        mats[i, 0] = high
        mats[i, 1] = (wide_mats[i] - high.astype(F32)).astype(BF16)
    for i in range(2):
        w_own(i).wait()

    def block_of(p):
        return pl.ds(pl.multiple_of(p * n_k, n_k), n_k)

    def send_section(q, r, n):
        at, to = pl.ds(r, n), pl.ds(t * local + lo * half + r, n)

        @pl.loop(1, 2 * n_tok)
        def _(j):
            p = (me + j * 27) % (2 * n_tok)
            remote(
                sec_out.at[q, at, p % 2, block_of(p // 2), :], sec_in.at[q, to],
                a_send.at[q], a_recv.at[q], (p // 2, (p % 2) * 2 + core),
            ).start()

        pltpu.make_async_copy(
            sec_out.at[q, at, lo, block_of(t), :], sec_in.at[q, to], a_own.at[q]
        ).start()

    def project(step):
        q = half // 2
        early = step < q
        middle = (step >= q) & (step < 2 * q)
        late = step - 2 * q
        r = jnp.where(early, step, jnp.where(middle, step - q, q + late // 2))
        other = jnp.where(early, 0, jnp.where(middle, 1, late % 2))
        l = lo + other - 2 * lo * other

        @pl.when(step == q)
        def _():
            for i in range(2):
                pltpu.make_async_copy(w.at[1 - lo, i], w.at[1 - lo, i], wr_sem.at[i]).wait()

        @pl.when(other == 0)
        def _():
            arrived(r, far, cross_r)
            forward(r).start()
            own(r).wait()
            arrived(r, near, core_r)
            arrived(r, far_core, fwd_r)

        row = jnp.concatenate([x[r, p] for p in range(pieces)], axis=1)
        value = dot(row, w[l, 0])
        gate = dot(row, w[l, 1])
        gated = (value * (gate / (1.0 + jnp.exp(-gate)))).astype(BF16)
        section = dot(first_mat[...], gated)
        for i in range(n_half):
            sec_out[i, r, l] = (section[:, i * LANES : (i + 1) * LANES] * twiddle_cols[r]).astype(BF16)

        @pl.when((other == 1) & (r % 2 == 1))
        def _():
            send_section(0, r - 1, 2)

    pl.loop(0, 2 * half)(project)
    for q in range(1, n_half):
        send_section(q, 0, half)

    most = pl.ds(0, n_a - half)
    step_a = 32
    quarter = local // 2

    def spread(q):
        lanes = pl.ds(pl.multiple_of(q * LANES, LANES), LANES)
        mine = sec_in.at[q, pl.ds(0, half)]
        pltpu.make_async_copy(mine, mine, a_own.at[q]).wait()
        pltpu.make_async_copy(sec_in.at[q, most], sec_in.at[q, most], a_recv.at[q]).wait()

        @pl.loop(0, n_a // step_a)
        def _(i):
            part = sec_in[q, pl.ds(i * step_a, step_a)].astype(F32)
            wide_in[pl.ds(pl.multiple_of(i * step_a * n_k, step_a * n_k), step_a * n_k), :] = part.reshape(
                step_a * n_k, LANES
            )

        @pl.loop(0, n_k // 2)
        def _(kp):
            two = [wide_in[pl.ds(2 * kp + i, n_a, stride=n_k), :].astype(BF16) for i in range(2)]
            two = jnp.concatenate(two, axis=1)
            mid = dot(mats[0, 0], two) + dot(mats[0, 1], two)
            scale = [freq_rows[2 * kp + i, q] * row_mat[:, lanes] for i in range(2)]
            mid = (mid * jnp.concatenate(scale, axis=1)).astype(BF16)
            end = dot(mats[1, 0], mid) + dot(mats[1, 1], mid)
            for i in range(2):
                wide_out[pl.ds(2 * kp + i, n_a, stride=n_k), :] = end[:, i * LANES : (i + 1) * LANES]

        for part in range(2):

            @pl.loop(0, n_tok)
            def _(j):
                pt = (t + j * 13) % n_tok
                first_row = pl.multiple_of(pt * local + part * quarter, quarter)
                rows_out = pl.ds(first_row, quarter)
                flat = pl.ds(pl.multiple_of(first_row * n_k, quarter * n_k), quarter * n_k)
                spec_out[q, rows_out] = wide_out[flat, :].astype(BF16).reshape(quarter, n_k, LANES)
                to = spec_in.at[q, pl.ds(part * quarter, quarter), block_of(t), :]

                @pl.when(j > 0)
                def _():
                    remote(
                        spec_out.at[q, rows_out], to, b_send.at[q, part], b_recv.at[q, part], (pt, h)
                    ).start()

                @pl.when(j == 0)
                def _():
                    pltpu.make_async_copy(spec_out.at[q, rows_out], to, b_own.at[q, part]).start()

    pl.loop(0, n_half)(spread)

    def both(ip):
        return pl.ds(pl.multiple_of(2 * ip * block, 2 * block), 2 * block)

    def finish(step):
        q, part = step // 2, step % 2
        lanes = pl.ds(pl.multiple_of(q * LANES, LANES), LANES)
        at = pl.ds(pl.multiple_of(part * quarter, quarter), quarter)
        mine = spec_in.at[q, at, pl.ds(0, n_k), :]
        rest = spec_in.at[q, at, pl.ds(0, (n_tok - 1) * n_k), :]
        pltpu.make_async_copy(mine, mine, b_own.at[q, part]).wait()
        pltpu.make_async_copy(rest, rest, b_recv.at[q, part]).wait()

        @pl.loop(0, quarter // 2)
        def _(i):
            ip = part * (quarter // 2) + i
            two = jnp.concatenate([spec_in[q, 2 * ip + i] for i in range(2)], axis=1)
            got = dot(mats[2, 0], two).astype(BF16)
            for i in range(2):
                here = pl.ds(pl.multiple_of((2 * ip + i) * block, block), block)
                result[here, lanes] = got[:, i * LANES : (i + 1) * LANES]

            @pl.when(q == n_half - 1)
            def _():
                pltpu.make_async_copy(result.at[both(ip)], out.at[both(ip)], out_sem.at[ip]).start()

    pl.loop(0, 2 * n_half)(finish)

    @pl.loop(0, half)
    def _(r):
        cross(r).wait_send()
        partner(r).wait_send()
        forward(r).wait_send()

    for i in range(2):
        w_far(i).wait_send()
    for q in range(n_half):
        pltpu.make_async_copy(sec_in.at[q, most], sec_in.at[q, most], a_send.at[q]).wait()
        for part in range(2):
            gone = spec_out.at[q, pl.ds(0, (n_tok - 1) * quarter)]
            pltpu.make_async_copy(gone, gone, b_send.at[q, part]).wait()

    @pl.loop(0, local // 2)
    def _(ip):
        pltpu.make_async_copy(result.at[both(ip)], out.at[both(ip)], out_sem.at[ip]).wait()


def shards(
    tokens,
    w_value,
    w_gate,
    first_factor,
    twiddle,
    second_factor,
    freq_kernel,
    row_kernel,
    inverse_first,
    inverse_second,
):
    n_tok = lax.axis_size("tok")
    tok_rows, width = tokens.shape
    block = first_factor.shape[0]
    depth = w_value.shape[0]
    n_a = second_factor.shape[0]
    local = tok_rows // block
    half = local // 2
    n_k = block // n_tok
    n_half = width // LANES
    hbm = pl.BlockSpec(memory_space=pl.ANY)
    dma = pltpu.SemaphoreType.DMA
    return pl.pallas_call(
        functools.partial(mixer, n_tok),
        out_shape=jax.ShapeDtypeStruct((tok_rows, width), BF16),
        in_specs=[hbm] * 10,
        out_specs=hbm,
        scratch_shapes=[
            pltpu.VMEM((half, depth // width, block, width), BF16),
            pltpu.VMEM((2, 2, depth, width), BF16),
            pltpu.VMEM((n_half, half, 2, block, LANES), BF16),
            pltpu.VMEM((n_half, n_a, n_k, LANES), BF16),
            pltpu.VMEM((n_a * n_k, LANES), F32),
            pltpu.VMEM((n_a * n_k, LANES), F32),
            pltpu.VMEM((n_half, n_a, n_k, LANES), BF16),
            pltpu.VMEM((n_half, local, block, LANES), BF16),
            pltpu.VMEM((tok_rows, width), BF16),
            pltpu.VMEM((3, n_a, n_a), F32),
            pltpu.VMEM((3, 2, n_a, n_a), BF16),
            pltpu.VMEM((block, block), BF16),
            pltpu.VMEM((local, block), F32),
            pltpu.VMEM((half, block, LANES), F32),
            pltpu.VMEM((n_k, width), F32),
            pltpu.VMEM((n_k, n_half, 1, LANES), F32),
            pltpu.VMEM((n_a, width), F32),
            dma((half,)), dma((half,)), dma((half,)), dma((half,)), dma((half,)), dma((half,)), dma((half,)),
            dma((2,)), dma((2,)), dma((2,)), dma((7,)),
            pltpu.SemaphoreType.REGULAR((n_tok.bit_length(),)),
            dma((n_half,)), dma((n_half,)), dma((n_half,)),
            dma((n_half, 2)), dma((n_half, 2)), dma((n_half, 2)), dma((local // 2,)),
        ],
        compiler_params=pltpu.CompilerParams(
            collective_id=0, has_side_effects=True, vmem_limit_bytes=63 * 2**20
        ),
    )(
        tokens, w_value, w_gate, first_factor, twiddle, second_factor, inverse_first, inverse_second,
        freq_kernel, row_kernel,
    )


def solution(mesh):
    return jax.shard_map(
        shards,
        mesh=mesh,
        in_specs=(
            P("tok", "ch"),
            P(None, "ch"),
            P(None, "ch"),
            P(),
            P("tok", None),
            P(),
            P("tok", "ch"),
            P(None, "ch"),
            P(),
            P(),
        ),
        out_specs=P("tok", "ch"),
        check_vma=False,
    )
```

```python
import functools

import jax
import jax.numpy as jnp
from jax import lax
from jax.experimental import pallas as pl
from jax.experimental.pallas import tpu as pltpu
from jax.sharding import PartitionSpec as P

MESH = pl.DeviceIdType.MESH
LANES = 128
F32, BF16 = jnp.float32, jnp.bfloat16


def dot(a, b):
    return jnp.dot(a, b, preferred_element_type=F32)


def flip(index, bit):
    return index + bit - 2 * bit * ((index // bit) % 2)


def mixer(
    n_tok,
    tokens, w_value, w_gate, first, twiddle, second, inv_one, inv_two, freq, row_kernel,
    out,
    x, w, sec_out, sec_in, wide_in, wide_out, spec_out, spec_in, result,
    wide_mats, mats, first_mat, twiddle_raw, twiddle_cols, freq_raw, freq_rows, row_mat,
    cross_s, cross_r, core_s, core_r, fwd_s, fwd_r, own_sem, w_sem, ws_sem, wr_sem, small_sem,
    known, a_send, a_recv, a_own, b_send, b_recv, b_own, out_sem,
):
    t, h = lax.axis_index("tok"), lax.axis_index("ch")
    lo, core = h // 2, h % 2
    half, pieces, block, width = x.shape
    n_half, n_a, n_k, _ = sec_in.shape
    local = 2 * half
    me = t * 2 + lo
    y_dev = (t, flip(h, 2))
    core_dev = (t, flip(h, 1))
    w_dev = (flip(t, 1), flip(h, 2))
    far, far_core, near = flip(h, 2), flip(flip(h, 2), 1), flip(h, 1)
    bits = [2**i for i in range(n_tok.bit_length() - 1)]
    links = [y_dev] + [(flip(t, b), h) for b in bits]

    barrier = pltpu.get_barrier_semaphore()
    close = links + [core_dev, w_dev]
    for d in close:
        pl.semaphore_signal(barrier, inc=1, device_id=d, device_id_type=MESH)

    def remote(src, dst, s, r, dev):
        return pltpu.make_async_remote_copy(
            src_ref=src, dst_ref=dst, send_sem=s, recv_sem=r, device_id=dev, device_id_type=MESH
        )

    def rows(at, r):
        return tokens.at[pl.ds(pl.multiple_of((at * half + r) * block, block), block), :]

    def cross(r):
        return remote(rows(1 - lo, r), x.at[r, h], cross_s.at[r], cross_r.at[r], y_dev)

    def partner(r):
        return remote(rows(lo, r), x.at[r, h], core_s.at[r], core_r.at[r], core_dev)

    def own(r):
        return pltpu.make_async_copy(rows(lo, r), x.at[r, h], own_sem.at[r])

    def forward(r):
        return remote(x.at[r, far], x.at[r, far], fwd_s.at[r], fwd_r.at[r], core_dev)

    def w_own(i):
        return pltpu.make_async_copy((w_value, w_gate)[i], w.at[lo, i], w_sem.at[i])

    def w_far(i):
        return remote((w_value, w_gate)[i], w.at[lo, i], ws_sem.at[i], wr_sem.at[i], w_dev)

    def arrived(r, piece, sem):
        pltpu.make_async_copy(x.at[r, piece], x.at[r, piece], sem.at[r]).wait()

    small = [
        (twiddle, twiddle_raw), (first, first_mat), (freq, freq_raw), (second, wide_mats.at[0]),
        (inv_one, wide_mats.at[1]), (inv_two, wide_mats.at[2]), (row_kernel, row_mat),
    ]
    loads = [pltpu.make_async_copy(a, b, small_sem.at[i]) for i, (a, b) in enumerate(small)]
    for i in range(2):
        w_own(i).start()
    for load in loads:
        load.start()

    pl.semaphore_wait(barrier, len(close))

    @pl.loop(0, half)
    def _(r):
        cross(r).start()

    for i in range(2):
        w_far(i).start()

    @pl.loop(0, half)
    def _(r):
        own(r).start()
        partner(r).start()

    for i, d in enumerate(links):
        pl.semaphore_signal(known.at[i], inc=1, device_id=d, device_id_type=MESH)
        pl.semaphore_wait(known.at[i], 1)

    for load in loads:
        load.wait()
    same = lax.broadcasted_iota(jnp.int32, (block, block), 0) == lax.broadcasted_iota(
        jnp.int32, (block, block), 1
    )

    @pl.loop(0, half)
    def _(r):
        row = twiddle_raw[pl.ds(pl.multiple_of(lo * half, half), half), :]
        pick = lax.broadcasted_iota(jnp.int32, row.shape, 0) == r
        row = jnp.sum(jnp.where(pick, row, 0.0), axis=0, keepdims=True)
        column = jnp.sum(jnp.where(same, row, 0.0), axis=1, keepdims=True)
        twiddle_cols[r] = jnp.broadcast_to(column, (block, LANES))

    for k in range(n_k):
        for q in range(n_half):
            freq_rows[k, q] = freq_raw[k : k + 1, q * LANES : (q + 1) * LANES]
    for i in range(3):
        high = wide_mats[i].astype(BF16)
        mats[i, 0] = high
        mats[i, 1] = (wide_mats[i] - high.astype(F32)).astype(BF16)
    for i in range(2):
        w_own(i).wait()

    def block_of(p):
        return pl.ds(pl.multiple_of(p * n_k, n_k), n_k)

    def send_section(q, r, n):
        at, to = pl.ds(r, n), pl.ds(t * local + lo * half + r, n)

        @pl.loop(1, 2 * n_tok)
        def _(j):
            p = (me + j * 27) % (2 * n_tok)
            remote(
                sec_out.at[q, at, p % 2, block_of(p // 2), :], sec_in.at[q, to],
                a_send.at[q], a_recv.at[q], (p // 2, (p % 2) * 2 + core),
            ).start()

        pltpu.make_async_copy(
            sec_out.at[q, at, lo, block_of(t), :], sec_in.at[q, to], a_own.at[q]
        ).start()

    def project(step):
        q = half // 2
        early = step < q
        middle = (step >= q) & (step < 2 * q)
        late = step - 2 * q
        r = jnp.where(early, step, jnp.where(middle, step - q, q + late // 2))
        other = jnp.where(early, 0, jnp.where(middle, 1, late % 2))
        l = lo + other - 2 * lo * other

        @pl.when(step == q)
        def _():
            for i in range(2):
                pltpu.make_async_copy(w.at[1 - lo, i], w.at[1 - lo, i], wr_sem.at[i]).wait()

        @pl.when(other == 0)
        def _():
            arrived(r, far, cross_r)
            forward(r).start()
            own(r).wait()
            arrived(r, near, core_r)
            arrived(r, far_core, fwd_r)

        row = jnp.concatenate([x[r, p] for p in range(pieces)], axis=1)
        value = dot(row, w[l, 0])
        gate = dot(row, w[l, 1])
        gated = (value * (gate / (1.0 + jnp.exp(-gate)))).astype(BF16)
        section = dot(first_mat[...], gated)
        for i in range(n_half):
            sec_out[i, r, l] = (section[:, i * LANES : (i + 1) * LANES] * twiddle_cols[r]).astype(BF16)

        @pl.when((other == 1) & (r % 2 == 1))
        def _():
            send_section(0, r - 1, 2)

    pl.loop(0, 2 * half)(project)
    for q in range(1, n_half):
        send_section(q, 0, half)

    most = pl.ds(0, n_a - half)
    step_a = 32
    quarter = local // 2

    def spread(q):
        lanes = pl.ds(pl.multiple_of(q * LANES, LANES), LANES)
        mine = sec_in.at[q, pl.ds(0, half)]
        pltpu.make_async_copy(mine, mine, a_own.at[q]).wait()
        pltpu.make_async_copy(sec_in.at[q, most], sec_in.at[q, most], a_recv.at[q]).wait()

        @pl.loop(0, n_a // step_a)
        def _(i):
            part = sec_in[q, pl.ds(i * step_a, step_a)].astype(F32)
            wide_in[pl.ds(pl.multiple_of(i * step_a * n_k, step_a * n_k), step_a * n_k), :] = part.reshape(
                step_a * n_k, LANES
            )

        @pl.loop(0, n_k // 2)
        def _(kp):
            two = [wide_in[pl.ds(2 * kp + i, n_a, stride=n_k), :].astype(BF16) for i in range(2)]
            two = jnp.concatenate(two, axis=1)
            mid = dot(mats[0, 0], two) + dot(mats[0, 1], two)
            scale = [freq_rows[2 * kp + i, q] * row_mat[:, lanes] for i in range(2)]
            mid = (mid * jnp.concatenate(scale, axis=1)).astype(BF16)
            end = dot(mats[1, 0], mid) + dot(mats[1, 1], mid)
            for i in range(2):
                wide_out[pl.ds(2 * kp + i, n_a, stride=n_k), :] = end[:, i * LANES : (i + 1) * LANES]

        for part in range(2):

            @pl.loop(0, n_tok)
            def _(j):
                pt = (t + j * 5) % n_tok
                first_row = pl.multiple_of(pt * local + part * quarter, quarter)
                rows_out = pl.ds(first_row, quarter)
                flat = pl.ds(pl.multiple_of(first_row * n_k, quarter * n_k), quarter * n_k)
                spec_out[q, rows_out] = wide_out[flat, :].astype(BF16).reshape(quarter, n_k, LANES)
                to = spec_in.at[q, pl.ds(part * quarter, quarter), block_of(t), :]

                @pl.when(j > 0)
                def _():
                    remote(
                        spec_out.at[q, rows_out], to, b_send.at[q, part], b_recv.at[q, part], (pt, h)
                    ).start()

                @pl.when(j == 0)
                def _():
                    pltpu.make_async_copy(spec_out.at[q, rows_out], to, b_own.at[q, part]).start()

    pl.loop(0, n_half)(spread)

    def both(ip):
        return pl.ds(pl.multiple_of(2 * ip * block, 2 * block), 2 * block)

    def finish(step):
        q, part = step // 2, step % 2
        lanes = pl.ds(pl.multiple_of(q * LANES, LANES), LANES)
        at = pl.ds(pl.multiple_of(part * quarter, quarter), quarter)
        mine = spec_in.at[q, at, pl.ds(0, n_k), :]
        rest = spec_in.at[q, at, pl.ds(0, (n_tok - 1) * n_k), :]
        pltpu.make_async_copy(mine, mine, b_own.at[q, part]).wait()
        pltpu.make_async_copy(rest, rest, b_recv.at[q, part]).wait()

        @pl.loop(0, quarter // 2)
        def _(i):
            ip = part * (quarter // 2) + i
            two = jnp.concatenate([spec_in[q, 2 * ip + i] for i in range(2)], axis=1)
            got = dot(mats[2, 0], two).astype(BF16)
            for i in range(2):
                here = pl.ds(pl.multiple_of((2 * ip + i) * block, block), block)
                result[here, lanes] = got[:, i * LANES : (i + 1) * LANES]

            @pl.when(q == n_half - 1)
            def _():
                pltpu.make_async_copy(result.at[both(ip)], out.at[both(ip)], out_sem.at[ip]).start()

    pl.loop(0, 2 * n_half)(finish)

    @pl.loop(0, half)
    def _(r):
        cross(r).wait_send()
        partner(r).wait_send()
        forward(r).wait_send()

    for i in range(2):
        w_far(i).wait_send()
    for q in range(n_half):
        pltpu.make_async_copy(sec_in.at[q, most], sec_in.at[q, most], a_send.at[q]).wait()
        for part in range(2):
            gone = spec_out.at[q, pl.ds(0, (n_tok - 1) * quarter)]
            pltpu.make_async_copy(gone, gone, b_send.at[q, part]).wait()

    @pl.loop(0, local // 2)
    def _(ip):
        pltpu.make_async_copy(result.at[both(ip)], out.at[both(ip)], out_sem.at[ip]).wait()


def shards(
    tokens,
    w_value,
    w_gate,
    first_factor,
    twiddle,
    second_factor,
    freq_kernel,
    row_kernel,
    inverse_first,
    inverse_second,
):
    n_tok = lax.axis_size("tok")
    tok_rows, width = tokens.shape
    block = first_factor.shape[0]
    depth = w_value.shape[0]
    n_a = second_factor.shape[0]
    local = tok_rows // block
    half = local // 2
    n_k = block // n_tok
    n_half = width // LANES
    hbm = pl.BlockSpec(memory_space=pl.ANY)
    dma = pltpu.SemaphoreType.DMA
    return pl.pallas_call(
        functools.partial(mixer, n_tok),
        out_shape=pltpu.VMEM((tok_rows, width), BF16),
        in_specs=[hbm] * 10,
        out_specs=hbm,
        scratch_shapes=[
            pltpu.VMEM((half, depth // width, block, width), BF16),
            pltpu.VMEM((2, 2, depth, width), BF16),
            pltpu.VMEM((n_half, half, 2, block, LANES), BF16),
            pltpu.VMEM((n_half, n_a, n_k, LANES), BF16),
            pltpu.VMEM((n_a * n_k, LANES), F32),
            pltpu.VMEM((n_a * n_k, LANES), F32),
            pltpu.VMEM((n_half, n_a, n_k, LANES), BF16),
            pltpu.VMEM((n_half, local, block, LANES), BF16),
            pltpu.VMEM((tok_rows, width), BF16),
            pltpu.VMEM((3, n_a, n_a), F32),
            pltpu.VMEM((3, 2, n_a, n_a), BF16),
            pltpu.VMEM((block, block), BF16),
            pltpu.VMEM((local, block), F32),
            pltpu.VMEM((half, block, LANES), F32),
            pltpu.VMEM((n_k, width), F32),
            pltpu.VMEM((n_k, n_half, 1, LANES), F32),
            pltpu.VMEM((n_a, width), F32),
            dma((half,)), dma((half,)), dma((half,)), dma((half,)), dma((half,)), dma((half,)), dma((half,)),
            dma((2,)), dma((2,)), dma((2,)), dma((7,)),
            pltpu.SemaphoreType.REGULAR((n_tok.bit_length(),)),
            dma((n_half,)), dma((n_half,)), dma((n_half,)),
            dma((n_half, 2)), dma((n_half, 2)), dma((n_half, 2)), dma((local // 2,)),
        ],
        compiler_params=pltpu.CompilerParams(
            collective_id=0, has_side_effects=True, vmem_limit_bytes=56 * 2**20
        ),
    )(
        tokens, w_value, w_gate, first_factor, twiddle, second_factor, inverse_first, inverse_second,
        freq_kernel, row_kernel,
    )


def solution(mesh):
    return jax.shard_map(
        shards,
        mesh=mesh,
        in_specs=(
            P("tok", "ch"),
            P(None, "ch"),
            P(None, "ch"),
            P(),
            P("tok", None),
            P(),
            P("tok", "ch"),
            P(None, "ch"),
            P(),
            P(),
        ),
        out_specs=P("tok", "ch"),
        check_vma=False,
    )
```

```python
import functools

import jax
import jax.numpy as jnp
from jax import lax
from jax.experimental import pallas as pl
from jax.experimental.pallas import tpu as pltpu
from jax.sharding import PartitionSpec as P

MESH = pl.DeviceIdType.MESH
LANES = 128
F32, BF16 = jnp.float32, jnp.bfloat16


def dot(a, b):
    return jnp.dot(a, b, preferred_element_type=F32)


def flip(index, bit):
    return index + bit - 2 * bit * ((index // bit) % 2)


def mixer(
    n_tok,
    tokens, w_value, w_gate, first, twiddle, second, inv_one, inv_two, freq, row_kernel,
    result,
    x, w, sec_out, sec_in, wide_in, wide_out, spec_out, spec_in,
    wide_mats, mats, first_mat, twiddle_raw, twiddle_cols, freq_raw, freq_rows, row_mat,
    cross_s, cross_r, core_s, core_r, fwd_s, fwd_r, own_sem, w_sem, ws_sem, wr_sem, small_sem,
    known, a_send, a_recv, a_own, b_send, b_recv, b_own,
):
    t, h = lax.axis_index("tok"), lax.axis_index("ch")
    lo, core = h // 2, h % 2
    half, pieces, block, width = x.shape
    n_half, n_a, n_k, _ = sec_in.shape
    local = 2 * half
    me = t * 2 + lo
    y_dev = (t, flip(h, 2))
    core_dev = (t, flip(h, 1))
    w_dev = (flip(t, 1), flip(h, 2))
    far, far_core, near = flip(h, 2), flip(flip(h, 2), 1), flip(h, 1)
    bits = [2**i for i in range(n_tok.bit_length() - 1)]
    links = [y_dev] + [(flip(t, b), h) for b in bits]

    barrier = pltpu.get_barrier_semaphore()
    close = links + [core_dev, w_dev]
    for d in close:
        pl.semaphore_signal(barrier, inc=1, device_id=d, device_id_type=MESH)

    def remote(src, dst, s, r, dev):
        return pltpu.make_async_remote_copy(
            src_ref=src, dst_ref=dst, send_sem=s, recv_sem=r, device_id=dev, device_id_type=MESH
        )

    def rows(at, r):
        return tokens.at[pl.ds(pl.multiple_of((at * half + r) * block, block), block), :]

    def cross(r):
        return remote(rows(1 - lo, r), x.at[r, h], cross_s.at[r], cross_r.at[r], y_dev)

    def partner(r):
        return remote(rows(lo, r), x.at[r, h], core_s.at[r], core_r.at[r], core_dev)

    def own(r):
        return pltpu.make_async_copy(rows(lo, r), x.at[r, h], own_sem.at[r])

    def forward(r):
        return remote(x.at[r, far], x.at[r, far], fwd_s.at[r], fwd_r.at[r], core_dev)

    def w_own(i):
        return pltpu.make_async_copy((w_value, w_gate)[i], w.at[lo, i], w_sem.at[i])

    def w_far(i):
        return remote((w_value, w_gate)[i], w.at[lo, i], ws_sem.at[i], wr_sem.at[i], w_dev)

    def arrived(r, piece, sem):
        pltpu.make_async_copy(x.at[r, piece], x.at[r, piece], sem.at[r]).wait()

    small = [
        (twiddle, twiddle_raw), (first, first_mat), (freq, freq_raw), (second, wide_mats.at[0]),
        (inv_one, wide_mats.at[1]), (inv_two, wide_mats.at[2]), (row_kernel, row_mat),
    ]
    loads = [pltpu.make_async_copy(a, b, small_sem.at[i]) for i, (a, b) in enumerate(small)]
    for i in range(2):
        w_own(i).start()
    for load in loads:
        load.start()

    pl.semaphore_wait(barrier, len(close))

    @pl.loop(0, half)
    def _(r):
        cross(r).start()

    for i in range(2):
        w_far(i).start()

    @pl.loop(0, half)
    def _(r):
        own(r).start()
        partner(r).start()

    for i, d in enumerate(links):
        pl.semaphore_signal(known.at[i], inc=1, device_id=d, device_id_type=MESH)
        pl.semaphore_wait(known.at[i], 1)

    for load in loads:
        load.wait()
    same = lax.broadcasted_iota(jnp.int32, (block, block), 0) == lax.broadcasted_iota(
        jnp.int32, (block, block), 1
    )

    @pl.loop(0, half)
    def _(r):
        row = twiddle_raw[pl.ds(pl.multiple_of(lo * half, half), half), :]
        pick = lax.broadcasted_iota(jnp.int32, row.shape, 0) == r
        row = jnp.sum(jnp.where(pick, row, 0.0), axis=0, keepdims=True)
        column = jnp.sum(jnp.where(same, row, 0.0), axis=1, keepdims=True)
        twiddle_cols[r] = jnp.broadcast_to(column, (block, LANES))

    for k in range(n_k):
        for q in range(n_half):
            freq_rows[k, q] = freq_raw[k : k + 1, q * LANES : (q + 1) * LANES]
    for i in range(3):
        high = wide_mats[i].astype(BF16)
        mats[i, 0] = high
        mats[i, 1] = (wide_mats[i] - high.astype(F32)).astype(BF16)
    for i in range(2):
        w_own(i).wait()

    def block_of(p):
        return pl.ds(pl.multiple_of(p * n_k, n_k), n_k)

    def send_section(q, r, n):
        at, to = pl.ds(r, n), pl.ds(t * local + lo * half + r, n)

        @pl.loop(1, 2 * n_tok)
        def _(j):
            p = (me + j * 27) % (2 * n_tok)
            remote(
                sec_out.at[q, at, p % 2, block_of(p // 2), :], sec_in.at[q, to],
                a_send.at[q], a_recv.at[q], (p // 2, (p % 2) * 2 + core),
            ).start()

        pltpu.make_async_copy(
            sec_out.at[q, at, lo, block_of(t), :], sec_in.at[q, to], a_own.at[q]
        ).start()

    def project(step):
        q = half // 2
        early = step < q
        middle = (step >= q) & (step < 2 * q)
        late = step - 2 * q
        r = jnp.where(early, step, jnp.where(middle, step - q, q + late // 2))
        other = jnp.where(early, 0, jnp.where(middle, 1, late % 2))
        l = lo + other - 2 * lo * other

        @pl.when(step == q)
        def _():
            for i in range(2):
                pltpu.make_async_copy(w.at[1 - lo, i], w.at[1 - lo, i], wr_sem.at[i]).wait()

        @pl.when(other == 0)
        def _():
            arrived(r, far, cross_r)
            forward(r).start()
            own(r).wait()
            arrived(r, near, core_r)
            arrived(r, far_core, fwd_r)

        row = jnp.concatenate([x[r, p] for p in range(pieces)], axis=1)
        value = dot(row, w[l, 0])
        gate = dot(row, w[l, 1])
        gated = (value * (gate / (1.0 + jnp.exp(-gate)))).astype(BF16)
        section = dot(first_mat[...], gated)
        for i in range(n_half):
            sec_out[i, r, l] = (section[:, i * LANES : (i + 1) * LANES] * twiddle_cols[r]).astype(BF16)

        @pl.when((other == 1) & (r % 2 == 1))
        def _():
            send_section(0, r - 1, 2)

    pl.loop(0, 2 * half)(project)
    for q in range(1, n_half):
        send_section(q, 0, half)

    most = pl.ds(0, n_a - half)
    step_a = 32
    n_part = b_send.shape[1]
    quarter = local // n_part

    def spread(q):
        lanes = pl.ds(pl.multiple_of(q * LANES, LANES), LANES)
        mine = sec_in.at[q, pl.ds(0, half)]
        pltpu.make_async_copy(mine, mine, a_own.at[q]).wait()
        pltpu.make_async_copy(sec_in.at[q, most], sec_in.at[q, most], a_recv.at[q]).wait()

        @pl.loop(0, n_a // step_a)
        def _(i):
            part = sec_in[q, pl.ds(i * step_a, step_a)].astype(F32)
            wide_in[pl.ds(pl.multiple_of(i * step_a * n_k, step_a * n_k), step_a * n_k), :] = part.reshape(
                step_a * n_k, LANES
            )

        @pl.loop(0, n_k // 2)
        def _(kp):
            two = [wide_in[pl.ds(2 * kp + i, n_a, stride=n_k), :].astype(BF16) for i in range(2)]
            two = jnp.concatenate(two, axis=1)
            mid = dot(mats[0, 0], two) + dot(mats[0, 1], two)
            scale = [freq_rows[2 * kp + i, q] * row_mat[:, lanes] for i in range(2)]
            mid = (mid * jnp.concatenate(scale, axis=1)).astype(BF16)
            end = dot(mats[1, 0], mid) + dot(mats[1, 1], mid)
            for i in range(2):
                wide_out[pl.ds(2 * kp + i, n_a, stride=n_k), :] = end[:, i * LANES : (i + 1) * LANES]

        for part in range(n_part):

            @pl.loop(0, n_tok)
            def _(j):
                pt = (t + j * 5) % n_tok
                first_row = pl.multiple_of(pt * local + part * quarter, quarter)
                rows_out = pl.ds(first_row, quarter)
                flat = pl.ds(pl.multiple_of(first_row * n_k, quarter * n_k), quarter * n_k)
                spec_out[q, rows_out] = wide_out[flat, :].astype(BF16).reshape(quarter, n_k, LANES)
                to = spec_in.at[q, pl.ds(part * quarter, quarter), block_of(t), :]

                @pl.when(j > 0)
                def _():
                    remote(
                        spec_out.at[q, rows_out], to, b_send.at[q, part], b_recv.at[q, part], (pt, h)
                    ).start()

                @pl.when(j == 0)
                def _():
                    pltpu.make_async_copy(spec_out.at[q, rows_out], to, b_own.at[q, part]).start()

    pl.loop(0, n_half)(spread)

    def finish(step):
        q, part = step // n_part, step % n_part
        lanes = pl.ds(pl.multiple_of(q * LANES, LANES), LANES)
        at = pl.ds(pl.multiple_of(part * quarter, quarter), quarter)
        mine = spec_in.at[q, at, pl.ds(0, n_k), :]
        rest = spec_in.at[q, at, pl.ds(0, (n_tok - 1) * n_k), :]
        pltpu.make_async_copy(mine, mine, b_own.at[q, part]).wait()
        pltpu.make_async_copy(rest, rest, b_recv.at[q, part]).wait()

        @pl.loop(0, quarter // 2)
        def _(i):
            ip = part * (quarter // 2) + i
            two = jnp.concatenate([spec_in[q, 2 * ip + i] for i in range(2)], axis=1)
            got = dot(mats[2, 0], two).astype(BF16)
            for i in range(2):
                here = pl.ds(pl.multiple_of((2 * ip + i) * block, block), block)
                result[here, lanes] = got[:, i * LANES : (i + 1) * LANES]

    pl.loop(0, n_part * n_half)(finish)

    @pl.loop(0, half)
    def _(r):
        cross(r).wait_send()
        partner(r).wait_send()
        forward(r).wait_send()

    for i in range(2):
        w_far(i).wait_send()
    for q in range(n_half):
        pltpu.make_async_copy(sec_in.at[q, most], sec_in.at[q, most], a_send.at[q]).wait()
        for part in range(n_part):
            gone = spec_out.at[q, pl.ds(0, (n_tok - 1) * quarter)]
            pltpu.make_async_copy(gone, gone, b_send.at[q, part]).wait()


def shards(
    tokens,
    w_value,
    w_gate,
    first_factor,
    twiddle,
    second_factor,
    freq_kernel,
    row_kernel,
    inverse_first,
    inverse_second,
):
    n_tok = lax.axis_size("tok")
    tok_rows, width = tokens.shape
    block = first_factor.shape[0]
    depth = w_value.shape[0]
    n_a = second_factor.shape[0]
    local = tok_rows // block
    half = local // 2
    n_k = block // n_tok
    n_half = width // LANES
    hbm = pl.BlockSpec(memory_space=pl.ANY)
    dma = pltpu.SemaphoreType.DMA
    return pl.pallas_call(
        functools.partial(mixer, n_tok),
        out_shape=pltpu.VMEM((tok_rows, width), BF16),
        in_specs=[hbm] * 10,
        out_specs=pl.BlockSpec(memory_space=pltpu.VMEM),
        scratch_shapes=[
            pltpu.VMEM((half, depth // width, block, width), BF16),
            pltpu.VMEM((2, 2, depth, width), BF16),
            pltpu.VMEM((n_half, half, 2, block, LANES), BF16),
            pltpu.VMEM((n_half, n_a, n_k, LANES), BF16),
            pltpu.VMEM((n_a * n_k, LANES), F32),
            pltpu.VMEM((n_a * n_k, LANES), F32),
            pltpu.VMEM((n_half, n_a, n_k, LANES), BF16),
            pltpu.VMEM((n_half, local, block, LANES), BF16),
            pltpu.VMEM((3, n_a, n_a), F32),
            pltpu.VMEM((3, 2, n_a, n_a), BF16),
            pltpu.VMEM((block, block), BF16),
            pltpu.VMEM((local, block), F32),
            pltpu.VMEM((half, block, LANES), F32),
            pltpu.VMEM((n_k, width), F32),
            pltpu.VMEM((n_k, n_half, 1, LANES), F32),
            pltpu.VMEM((n_a, width), F32),
            dma((half,)), dma((half,)), dma((half,)), dma((half,)), dma((half,)), dma((half,)), dma((half,)),
            dma((2,)), dma((2,)), dma((2,)), dma((7,)),
            pltpu.SemaphoreType.REGULAR((n_tok.bit_length(),)),
            dma((n_half,)), dma((n_half,)), dma((n_half,)),
            dma((n_half, 4)), dma((n_half, 4)), dma((n_half, 4)),
        ],
        compiler_params=pltpu.CompilerParams(
            collective_id=0, has_side_effects=True, vmem_limit_bytes=52 * 2**20
        ),
    )(
        tokens, w_value, w_gate, first_factor, twiddle, second_factor, inverse_first, inverse_second,
        freq_kernel, row_kernel,
    )


def solution(mesh):
    return jax.shard_map(
        shards,
        mesh=mesh,
        in_specs=(
            P("tok", "ch"),
            P(None, "ch"),
            P(None, "ch"),
            P(),
            P("tok", None),
            P(),
            P("tok", "ch"),
            P(None, "ch"),
            P(),
            P(),
        ),
        out_specs=P("tok", "ch"),
        check_vma=False,
    )
```

```python
import functools

import jax
import jax.numpy as jnp
from jax import lax
from jax.experimental import pallas as pl
from jax.experimental.pallas import tpu as pltpu
from jax.sharding import PartitionSpec as P

MESH = pl.DeviceIdType.MESH
LANES = 128
F32, BF16 = jnp.float32, jnp.bfloat16


def dot(a, b):
    return jnp.dot(a, b, preferred_element_type=F32)


def flip(index, bit):
    return index + bit - 2 * bit * ((index // bit) % 2)


def mixer(
    n_tok,
    tokens, w_value, w_gate, first, twiddle, second, inv_one, inv_two, freq, row_kernel,
    result,
    x, w, sec_out, sec_in, wide_in, wide_out, spec_out, spec_in,
    wide_mats, mats, first_mat, twiddle_raw, twiddle_cols, freq_raw, freq_rows, row_mat,
    cross_s, cross_r, core_s, core_r, fwd_s, fwd_r, own_sem, w_sem, ws_sem, wr_sem, small_sem,
    known, a_send, a_recv, a_own, b_send, b_recv, b_own,
):
    t, h = lax.axis_index("tok"), lax.axis_index("ch")
    lo, core = h // 2, h % 2
    half, pieces, block, width = x.shape
    n_half, n_a, n_k, _ = sec_in.shape
    local = 2 * half
    me = t * 2 + lo
    y_dev = (t, flip(h, 2))
    core_dev = (t, flip(h, 1))
    w_dev = (flip(t, 1), flip(h, 2))
    far, far_core, near = flip(h, 2), flip(flip(h, 2), 1), flip(h, 1)
    bits = [2**i for i in range(n_tok.bit_length() - 1)]
    links = [y_dev] + [(flip(t, b), h) for b in bits]

    barrier = pltpu.get_barrier_semaphore()
    close = links + [core_dev, w_dev]
    for d in close:
        pl.semaphore_signal(barrier, inc=1, device_id=d, device_id_type=MESH)

    def remote(src, dst, s, r, dev):
        return pltpu.make_async_remote_copy(
            src_ref=src, dst_ref=dst, send_sem=s, recv_sem=r, device_id=dev, device_id_type=MESH
        )

    def rows(at, r):
        return tokens.at[pl.ds(pl.multiple_of((at * half + r) * block, block), block), :]

    def cross(r):
        return remote(rows(1 - lo, r), x.at[r, h], cross_s.at[r], cross_r.at[r], y_dev)

    def partner(r):
        return remote(rows(lo, r), x.at[r, h], core_s.at[r], core_r.at[r], core_dev)

    def own(r):
        return pltpu.make_async_copy(rows(lo, r), x.at[r, h], own_sem.at[r])

    def forward(r):
        return remote(x.at[r, far], x.at[r, far], fwd_s.at[r], fwd_r.at[r], core_dev)

    def w_own(i):
        return pltpu.make_async_copy((w_value, w_gate)[i], w.at[lo, i], w_sem.at[i])

    def w_far(i):
        return remote((w_value, w_gate)[i], w.at[lo, i], ws_sem.at[i], wr_sem.at[i], w_dev)

    def arrived(r, piece, sem):
        pltpu.make_async_copy(x.at[r, piece], x.at[r, piece], sem.at[r]).wait()

    small = [
        (twiddle, twiddle_raw), (first, first_mat), (freq, freq_raw), (second, wide_mats.at[0]),
        (inv_one, wide_mats.at[1]), (inv_two, wide_mats.at[2]), (row_kernel, row_mat),
    ]
    loads = [pltpu.make_async_copy(a, b, small_sem.at[i]) for i, (a, b) in enumerate(small)]
    for i in range(2):
        w_own(i).start()
    for load in loads:
        load.start()

    pl.semaphore_wait(barrier, len(close))

    @pl.loop(0, half)
    def _(r):
        cross(r).start()

    for i in range(2):
        w_far(i).start()

    @pl.loop(0, half)
    def _(r):
        own(r).start()
        partner(r).start()

    for load in loads:
        load.wait()
    same = lax.broadcasted_iota(jnp.int32, (block, block), 0) == lax.broadcasted_iota(
        jnp.int32, (block, block), 1
    )

    @pl.loop(0, half)
    def _(r):
        row = twiddle_raw[pl.ds(pl.multiple_of(lo * half, half), half), :]
        pick = lax.broadcasted_iota(jnp.int32, row.shape, 0) == r
        row = jnp.sum(jnp.where(pick, row, 0.0), axis=0, keepdims=True)
        column = jnp.sum(jnp.where(same, row, 0.0), axis=1, keepdims=True)
        twiddle_cols[r] = jnp.broadcast_to(column, (block, LANES))

    for k in range(n_k):
        for q in range(n_half):
            freq_rows[k, q] = freq_raw[k : k + 1, q * LANES : (q + 1) * LANES]
    for i in range(3):
        high = wide_mats[i].astype(BF16)
        mats[i, 0] = high
        mats[i, 1] = (wide_mats[i] - high.astype(F32)).astype(BF16)
    for i in range(2):
        w_own(i).wait()

    for i, d in enumerate(links):
        pl.semaphore_signal(known.at[i], inc=1, device_id=d, device_id_type=MESH)
        pl.semaphore_wait(known.at[i], 1)

    def block_of(p):
        return pl.ds(pl.multiple_of(p * n_k, n_k), n_k)

    def send_section(q, r, n):
        at, to = pl.ds(r, n), pl.ds(t * local + lo * half + r, n)

        @pl.loop(1, 2 * n_tok)
        def _(j):
            p = (me + j * 39) % (2 * n_tok)
            remote(
                sec_out.at[q, at, p % 2, block_of(p // 2), :], sec_in.at[q, to],
                a_send.at[q], a_recv.at[q], (p // 2, (p % 2) * 2 + core),
            ).start()

        pltpu.make_async_copy(
            sec_out.at[q, at, lo, block_of(t), :], sec_in.at[q, to], a_own.at[q]
        ).start()

    def project(step):
        q = half * 3 // 8
        early = step < q
        middle = (step >= q) & (step < 2 * q)
        late = step - 2 * q
        r = jnp.where(early, step, jnp.where(middle, step - q, q + late // 2))
        other = jnp.where(early, 0, jnp.where(middle, 1, late % 2))
        l = lo + other - 2 * lo * other

        @pl.when(step == q)
        def _():
            for i in range(2):
                pltpu.make_async_copy(w.at[1 - lo, i], w.at[1 - lo, i], wr_sem.at[i]).wait()

        @pl.when(other == 0)
        def _():
            arrived(r, far, cross_r)
            forward(r).start()
            own(r).wait()
            arrived(r, near, core_r)
            arrived(r, far_core, fwd_r)

        row = jnp.concatenate([x[r, p] for p in range(pieces)], axis=1)
        value = dot(row, w[l, 0])
        gate = dot(row, w[l, 1])
        gated = (value * (gate / (1.0 + jnp.exp(-gate)))).astype(BF16)
        section = dot(first_mat[...], gated)
        for i in range(n_half):
            sec_out[i, r, l] = (section[:, i * LANES : (i + 1) * LANES] * twiddle_cols[r]).astype(BF16)

        @pl.when((other == 1) & (r % 2 == 1))
        def _():
            send_section(0, r - 1, 2)

    pl.loop(0, 2 * half)(project)
    for q in range(1, n_half):
        send_section(q, 0, half)

    most = pl.ds(0, n_a - half)
    step_a = 64
    n_part = b_send.shape[1]
    quarter = local // n_part

    def spread(q):
        lanes = pl.ds(pl.multiple_of(q * LANES, LANES), LANES)
        mine = sec_in.at[q, pl.ds(0, half)]
        pltpu.make_async_copy(mine, mine, a_own.at[q]).wait()
        pltpu.make_async_copy(sec_in.at[q, most], sec_in.at[q, most], a_recv.at[q]).wait()

        @pl.loop(0, n_a // step_a)
        def _(i):
            part = sec_in[q, pl.ds(i * step_a, step_a)].astype(F32)
            wide_in[pl.ds(pl.multiple_of(i * step_a * n_k, step_a * n_k), step_a * n_k), :] = part.reshape(
                step_a * n_k, LANES
            )

        @pl.loop(0, n_k // 2)
        def _(kp):
            two = [wide_in[pl.ds(2 * kp + i, n_a, stride=n_k), :].astype(BF16) for i in range(2)]
            two = jnp.concatenate(two, axis=1)
            mid = dot(mats[0, 0], two) + dot(mats[0, 1], two)
            scale = [freq_rows[2 * kp + i, q] * row_mat[:, lanes] for i in range(2)]
            mid = (mid * jnp.concatenate(scale, axis=1)).astype(BF16)
            end = dot(mats[1, 0], mid) + dot(mats[1, 1], mid)
            for i in range(2):
                wide_out[pl.ds(2 * kp + i, n_a, stride=n_k), :] = end[:, i * LANES : (i + 1) * LANES]

        for part in range(n_part):

            @pl.loop(0, n_tok)
            def _(j):
                pt = (t + j * 5) % n_tok
                first_row = pl.multiple_of(pt * local + part * quarter, quarter)
                rows_out = pl.ds(first_row, quarter)
                flat = pl.ds(pl.multiple_of(first_row * n_k, quarter * n_k), quarter * n_k)
                spec_out[q, rows_out] = wide_out[flat, :].astype(BF16).reshape(quarter, n_k, LANES)
                to = spec_in.at[q, pl.ds(part * quarter, quarter), block_of(t), :]

                @pl.when(j > 0)
                def _():
                    remote(
                        spec_out.at[q, rows_out], to, b_send.at[q, part], b_recv.at[q, part], (pt, h)
                    ).start()

                @pl.when(j == 0)
                def _():
                    pltpu.make_async_copy(spec_out.at[q, rows_out], to, b_own.at[q, part]).start()

    pl.loop(0, n_half)(spread)

    def finish(step):
        q, part = step // n_part, step % n_part
        lanes = pl.ds(pl.multiple_of(q * LANES, LANES), LANES)
        at = pl.ds(pl.multiple_of(part * quarter, quarter), quarter)
        mine = spec_in.at[q, at, pl.ds(0, n_k), :]
        rest = spec_in.at[q, at, pl.ds(0, (n_tok - 1) * n_k), :]
        pltpu.make_async_copy(mine, mine, b_own.at[q, part]).wait()
        pltpu.make_async_copy(rest, rest, b_recv.at[q, part]).wait()

        @pl.loop(0, quarter // 2)
        def _(i):
            ip = part * (quarter // 2) + i
            two = jnp.concatenate([spec_in[q, 2 * ip + i] for i in range(2)], axis=1)
            got = dot(mats[2, 0], two).astype(BF16)
            for i in range(2):
                here = pl.ds(pl.multiple_of((2 * ip + i) * block, block), block)
                result[here, lanes] = got[:, i * LANES : (i + 1) * LANES]

    pl.loop(0, n_part * n_half)(finish)

    @pl.loop(0, half)
    def _(r):
        cross(r).wait_send()
        partner(r).wait_send()
        forward(r).wait_send()

    for i in range(2):
        w_far(i).wait_send()
    for q in range(n_half):
        pltpu.make_async_copy(sec_in.at[q, most], sec_in.at[q, most], a_send.at[q]).wait()
        for part in range(n_part):
            gone = spec_out.at[q, pl.ds(0, (n_tok - 1) * quarter)]
            pltpu.make_async_copy(gone, gone, b_send.at[q, part]).wait()


def shards(
    tokens,
    w_value,
    w_gate,
    first_factor,
    twiddle,
    second_factor,
    freq_kernel,
    row_kernel,
    inverse_first,
    inverse_second,
):
    n_tok = lax.axis_size("tok")
    tok_rows, width = tokens.shape
    block = first_factor.shape[0]
    depth = w_value.shape[0]
    n_a = second_factor.shape[0]
    local = tok_rows // block
    half = local // 2
    n_k = block // n_tok
    n_half = width // LANES
    hbm = pl.BlockSpec(memory_space=pl.ANY)
    dma = pltpu.SemaphoreType.DMA
    return pl.pallas_call(
        functools.partial(mixer, n_tok),
        out_shape=pltpu.VMEM((tok_rows, width), BF16),
        in_specs=[hbm] * 10,
        out_specs=pl.BlockSpec(memory_space=pltpu.VMEM),
        scratch_shapes=[
            pltpu.VMEM((half, depth // width, block, width), BF16),
            pltpu.VMEM((2, 2, depth, width), BF16),
            pltpu.VMEM((n_half, half, 2, block, LANES), BF16),
            pltpu.VMEM((n_half, n_a, n_k, LANES), BF16),
            pltpu.VMEM((n_a * n_k, LANES), F32),
            pltpu.VMEM((n_a * n_k, LANES), F32),
            pltpu.VMEM((n_half, n_a, n_k, LANES), BF16),
            pltpu.VMEM((n_half, local, block, LANES), BF16),
            pltpu.VMEM((3, n_a, n_a), F32),
            pltpu.VMEM((3, 2, n_a, n_a), BF16),
            pltpu.VMEM((block, block), BF16),
            pltpu.VMEM((local, block), F32),
            pltpu.VMEM((half, block, LANES), F32),
            pltpu.VMEM((n_k, width), F32),
            pltpu.VMEM((n_k, n_half, 1, LANES), F32),
            pltpu.VMEM((n_a, width), F32),
            dma((half,)), dma((half,)), dma((half,)), dma((half,)), dma((half,)), dma((half,)), dma((half,)),
            dma((2,)), dma((2,)), dma((2,)), dma((7,)),
            pltpu.SemaphoreType.REGULAR((n_tok.bit_length(),)),
            dma((n_half,)), dma((n_half,)), dma((n_half,)),
            dma((n_half, 4)), dma((n_half, 4)), dma((n_half, 4)),
        ],
        compiler_params=pltpu.CompilerParams(
            collective_id=0, has_side_effects=True, vmem_limit_bytes=52 * 2**20
        ),
    )(
        tokens, w_value, w_gate, first_factor, twiddle, second_factor, inverse_first, inverse_second,
        freq_kernel, row_kernel,
    )


def solution(mesh):
    return jax.shard_map(
        shards,
        mesh=mesh,
        in_specs=(
            P("tok", "ch"),
            P(None, "ch"),
            P(None, "ch"),
            P(),
            P("tok", None),
            P(),
            P("tok", "ch"),
            P(None, "ch"),
            P(),
            P(),
        ),
        out_specs=P("tok", "ch"),
        check_vma=False,
    )
```

```python
import functools

import jax
import jax.numpy as jnp
from jax import lax
from jax.experimental import pallas as pl
from jax.experimental.pallas import tpu as pltpu
from jax.sharding import PartitionSpec as P

MESH = pl.DeviceIdType.MESH
LANES = 128
F32, BF16 = jnp.float32, jnp.bfloat16


def dot(a, b):
    return jnp.dot(a, b, preferred_element_type=F32)


def flip(index, bit):
    return index + bit - 2 * bit * ((index // bit) % 2)


def mixer(
    n_tok,
    tokens, w_value, w_gate, first, twiddle, second, inv_one, inv_two, freq, row_kernel,
    result,
    x, w, sec_out, sec_in, wide_in, wide_out, spec_out, spec_in,
    wide_mats, mats, first_mat, twiddle_raw, twiddle_cols, freq_raw, freq_rows, row_mat,
    cross_s, cross_r, core_s, core_r, fwd_s, fwd_r, own_sem, w_sem, ws_sem, wr_sem, small_sem,
    known, a_send, a_recv, a_own, b_send, b_recv, b_own,
):
    t, h = lax.axis_index("tok"), lax.axis_index("ch")
    lo, core = h // 2, h % 2
    half, pieces, block, width = x.shape
    n_half, n_a, n_k, _ = sec_in.shape
    local = 2 * half
    me = t * 2 + lo
    y_dev = (t, flip(h, 2))
    core_dev = (t, flip(h, 1))
    w_dev = (flip(t, 1), flip(h, 2))
    far, far_core, near = flip(h, 2), flip(flip(h, 2), 1), flip(h, 1)
    bits = [2**i for i in range(n_tok.bit_length() - 1)]
    links = [y_dev] + [(flip(t, b), h) for b in bits]

    barrier = pltpu.get_barrier_semaphore()
    close = links + [core_dev, w_dev]
    for d in close:
        pl.semaphore_signal(barrier, inc=1, device_id=d, device_id_type=MESH)

    def remote(src, dst, s, r, dev):
        return pltpu.make_async_remote_copy(
            src_ref=src, dst_ref=dst, send_sem=s, recv_sem=r, device_id=dev, device_id_type=MESH
        )

    def rows(at, r):
        return tokens.at[pl.ds(pl.multiple_of((at * half + r) * block, block), block), :]

    def cross(r):
        return remote(rows(1 - lo, r), x.at[r, h], cross_s.at[r], cross_r.at[r], y_dev)

    def partner(r):
        return remote(rows(lo, r), x.at[r, h], core_s.at[r], core_r.at[r], core_dev)

    def own(r):
        return pltpu.make_async_copy(rows(lo, r), x.at[r, h], own_sem.at[r])

    def forward(r):
        return remote(x.at[r, far], x.at[r, far], fwd_s.at[r], fwd_r.at[r], core_dev)

    def w_own(i):
        return pltpu.make_async_copy((w_value, w_gate)[i], w.at[lo, i], w_sem.at[i])

    def w_far(i):
        return remote((w_value, w_gate)[i], w.at[lo, i], ws_sem.at[i], wr_sem.at[i], w_dev)

    def arrived(r, piece, sem):
        pltpu.make_async_copy(x.at[r, piece], x.at[r, piece], sem.at[r]).wait()

    small = [
        (twiddle, twiddle_raw), (first, first_mat), (freq, freq_raw), (second, wide_mats.at[0]),
        (inv_one, wide_mats.at[1]), (inv_two, wide_mats.at[2]), (row_kernel, row_mat),
    ]
    loads = [pltpu.make_async_copy(a, b, small_sem.at[i]) for i, (a, b) in enumerate(small)]
    for i in range(2):
        w_own(i).start()
    for load in loads:
        load.start()

    pl.semaphore_wait(barrier, len(close))

    for i in range(2):
        w_far(i).start()

    @pl.loop(0, half)
    def _(r):
        cross(r).start()

    @pl.loop(0, half)
    def _(r):
        own(r).start()
        partner(r).start()

    for load in loads:
        load.wait()
    same = lax.broadcasted_iota(jnp.int32, (block, block), 0) == lax.broadcasted_iota(
        jnp.int32, (block, block), 1
    )

    @pl.loop(0, half)
    def _(r):
        row = twiddle_raw[pl.ds(pl.multiple_of(lo * half, half), half), :]
        pick = lax.broadcasted_iota(jnp.int32, row.shape, 0) == r
        row = jnp.sum(jnp.where(pick, row, 0.0), axis=0, keepdims=True)
        column = jnp.sum(jnp.where(same, row, 0.0), axis=1, keepdims=True)
        twiddle_cols[r] = jnp.broadcast_to(column, (block, LANES))

    for k in range(n_k):
        for q in range(n_half):
            freq_rows[k, q] = freq_raw[k : k + 1, q * LANES : (q + 1) * LANES]
    for i in range(3):
        high = wide_mats[i].astype(BF16)
        mats[i, 0] = high
        mats[i, 1] = (wide_mats[i] - high.astype(F32)).astype(BF16)
    for i in range(2):
        w_own(i).wait()

    for i, d in enumerate(links):
        pl.semaphore_signal(known.at[i], inc=1, device_id=d, device_id_type=MESH)
        pl.semaphore_wait(known.at[i], 1)

    def block_of(p):
        return pl.ds(pl.multiple_of(p * n_k, n_k), n_k)

    def send_section(q, r, n):
        at, to = pl.ds(r, n), pl.ds(t * local + lo * half + r, n)

        @pl.loop(1, 2 * n_tok)
        def _(j):
            p = (me + j * 39) % (2 * n_tok)
            remote(
                sec_out.at[q, at, p % 2, block_of(p // 2), :], sec_in.at[q, to],
                a_send.at[q], a_recv.at[q], (p // 2, (p % 2) * 2 + core),
            ).start()

        pltpu.make_async_copy(
            sec_out.at[q, at, lo, block_of(t), :], sec_in.at[q, to], a_own.at[q]
        ).start()

    def project(step):
        q = half * 3 // 8
        early = step < q
        middle = (step >= q) & (step < 2 * q)
        late = step - 2 * q
        r = jnp.where(early, step, jnp.where(middle, step - q, q + late // 2))
        other = jnp.where(early, 0, jnp.where(middle, 1, late % 2))
        l = lo + other - 2 * lo * other

        @pl.when(step == q)
        def _():
            for i in range(2):
                pltpu.make_async_copy(w.at[1 - lo, i], w.at[1 - lo, i], wr_sem.at[i]).wait()

        @pl.when(other == 0)
        def _():
            arrived(r, far, cross_r)
            forward(r).start()
            own(r).wait()
            arrived(r, near, core_r)
            arrived(r, far_core, fwd_r)

        row = jnp.concatenate([x[r, p] for p in range(pieces)], axis=1)
        value = dot(row, w[l, 0])
        gate = dot(row, w[l, 1])
        gated = (value * (gate / (1.0 + jnp.exp(-gate)))).astype(BF16)
        section = dot(first_mat[...], gated)
        for i in range(n_half):
            sec_out[i, r, l] = (section[:, i * LANES : (i + 1) * LANES] * twiddle_cols[r]).astype(BF16)

        @pl.when((other == 1) & (r % 2 == 1))
        def _():
            send_section(0, r - 1, 2)

    pl.loop(0, 2 * half)(project)
    for q in range(1, n_half):
        send_section(q, 0, half)

    most = pl.ds(0, n_a - half)
    step_a = 64
    n_part = b_send.shape[1]
    quarter = local // n_part

    def spread(q):
        lanes = pl.ds(pl.multiple_of(q * LANES, LANES), LANES)
        mine = sec_in.at[q, pl.ds(0, half)]
        pltpu.make_async_copy(mine, mine, a_own.at[q]).wait()
        pltpu.make_async_copy(sec_in.at[q, most], sec_in.at[q, most], a_recv.at[q]).wait()

        @pl.loop(0, n_a // step_a)
        def _(i):
            part = sec_in[q, pl.ds(i * step_a, step_a)].astype(F32)
            wide_in[pl.ds(pl.multiple_of(i * step_a * n_k, step_a * n_k), step_a * n_k), :] = part.reshape(
                step_a * n_k, LANES
            )

        @pl.loop(0, n_k // 2)
        def _(kp):
            two = [wide_in[pl.ds(2 * kp + i, n_a, stride=n_k), :].astype(BF16) for i in range(2)]
            two = jnp.concatenate(two, axis=1)
            mid = dot(mats[0, 0], two) + dot(mats[0, 1], two)
            scale = [freq_rows[2 * kp + i, q] * row_mat[:, lanes] for i in range(2)]
            mid = (mid * jnp.concatenate(scale, axis=1)).astype(BF16)
            end = dot(mats[1, 0], mid) + dot(mats[1, 1], mid)
            for i in range(2):
                wide_out[pl.ds(2 * kp + i, n_a, stride=n_k), :] = end[:, i * LANES : (i + 1) * LANES]

        for part in range(n_part):

            @pl.loop(0, n_tok)
            def _(j):
                pt = (t + j * 5) % n_tok
                first_row = pl.multiple_of(pt * local + part * quarter, quarter)
                rows_out = pl.ds(first_row, quarter)
                flat = pl.ds(pl.multiple_of(first_row * n_k, quarter * n_k), quarter * n_k)
                spec_out[q, rows_out] = wide_out[flat, :].astype(BF16).reshape(quarter, n_k, LANES)
                to = spec_in.at[q, pl.ds(part * quarter, quarter), block_of(t), :]

                @pl.when(j > 0)
                def _():
                    remote(
                        spec_out.at[q, rows_out], to, b_send.at[q, part], b_recv.at[q, part], (pt, h)
                    ).start()

                @pl.when(j == 0)
                def _():
                    pltpu.make_async_copy(spec_out.at[q, rows_out], to, b_own.at[q, part]).start()

    pl.loop(0, n_half)(spread)

    def finish(step):
        q, part = step // n_part, step % n_part
        lanes = pl.ds(pl.multiple_of(q * LANES, LANES), LANES)
        at = pl.ds(pl.multiple_of(part * quarter, quarter), quarter)
        mine = spec_in.at[q, at, pl.ds(0, n_k), :]
        rest = spec_in.at[q, at, pl.ds(0, (n_tok - 1) * n_k), :]
        pltpu.make_async_copy(mine, mine, b_own.at[q, part]).wait()
        pltpu.make_async_copy(rest, rest, b_recv.at[q, part]).wait()

        @pl.loop(0, quarter // 2)
        def _(i):
            ip = part * (quarter // 2) + i
            two = jnp.concatenate([spec_in[q, 2 * ip + i] for i in range(2)], axis=1)
            got = dot(mats[2, 0], two).astype(BF16)
            for i in range(2):
                here = pl.ds(pl.multiple_of((2 * ip + i) * block, block), block)
                result[here, lanes] = got[:, i * LANES : (i + 1) * LANES]

    pl.loop(0, n_part * n_half)(finish)

    @pl.loop(0, half)
    def _(r):
        cross(r).wait_send()
        partner(r).wait_send()
        forward(r).wait_send()

    for i in range(2):
        w_far(i).wait_send()
    for q in range(n_half):
        pltpu.make_async_copy(sec_in.at[q, most], sec_in.at[q, most], a_send.at[q]).wait()
        for part in range(n_part):
            gone = spec_out.at[q, pl.ds(0, (n_tok - 1) * quarter)]
            pltpu.make_async_copy(gone, gone, b_send.at[q, part]).wait()


def shards(
    tokens,
    w_value,
    w_gate,
    first_factor,
    twiddle,
    second_factor,
    freq_kernel,
    row_kernel,
    inverse_first,
    inverse_second,
):
    n_tok = lax.axis_size("tok")
    tok_rows, width = tokens.shape
    block = first_factor.shape[0]
    depth = w_value.shape[0]
    n_a = second_factor.shape[0]
    local = tok_rows // block
    half = local // 2
    n_k = block // n_tok
    n_half = width // LANES
    hbm = pl.BlockSpec(memory_space=pl.ANY)
    dma = pltpu.SemaphoreType.DMA
    return pl.pallas_call(
        functools.partial(mixer, n_tok),
        out_shape=pltpu.VMEM((tok_rows, width), BF16),
        in_specs=[hbm] * 10,
        out_specs=pl.BlockSpec(memory_space=pltpu.VMEM),
        scratch_shapes=[
            pltpu.VMEM((half, depth // width, block, width), BF16),
            pltpu.VMEM((2, 2, depth, width), BF16),
            pltpu.VMEM((n_half, half, 2, block, LANES), BF16),
            pltpu.VMEM((n_half, n_a, n_k, LANES), BF16),
            pltpu.VMEM((n_a * n_k, LANES), F32),
            pltpu.VMEM((n_a * n_k, LANES), F32),
            pltpu.VMEM((n_half, n_a, n_k, LANES), BF16),
            pltpu.VMEM((n_half, local, block, LANES), BF16),
            pltpu.VMEM((3, n_a, n_a), F32),
            pltpu.VMEM((3, 2, n_a, n_a), BF16),
            pltpu.VMEM((block, block), BF16),
            pltpu.VMEM((local, block), F32),
            pltpu.VMEM((half, block, LANES), F32),
            pltpu.VMEM((n_k, width), F32),
            pltpu.VMEM((n_k, n_half, 1, LANES), F32),
            pltpu.VMEM((n_a, width), F32),
            dma((half,)), dma((half,)), dma((half,)), dma((half,)), dma((half,)), dma((half,)), dma((half,)),
            dma((2,)), dma((2,)), dma((2,)), dma((7,)),
            pltpu.SemaphoreType.REGULAR((n_tok.bit_length(),)),
            dma((n_half,)), dma((n_half,)), dma((n_half,)),
            dma((n_half, 4)), dma((n_half, 4)), dma((n_half, 4)),
        ],
        compiler_params=pltpu.CompilerParams(
            collective_id=0, has_side_effects=True, vmem_limit_bytes=52 * 2**20
        ),
    )(
        tokens, w_value, w_gate, first_factor, twiddle, second_factor, inverse_first, inverse_second,
        freq_kernel, row_kernel,
    )


def solution(mesh):
    return jax.shard_map(
        shards,
        mesh=mesh,
        in_specs=(
            P("tok", "ch"),
            P(None, "ch"),
            P(None, "ch"),
            P(),
            P("tok", None),
            P(),
            P("tok", "ch"),
            P(None, "ch"),
            P(),
            P(),
        ),
        out_specs=P("tok", "ch"),
        check_vma=False,
    )
```
